32 devices in a mesh: seq: 16 (over z, y, x), chan: 2 (over core).
Axes of the slice: x: 2, y: 2, z: 4, core: 2. Of those that a mesh axis runs over, the one named last changes fastest.
Arguments:
- values: bfloat16 [256, 8192], P('chan', 'seq'), may hold values from -6 to 6
- gate_one: bfloat16 [256, 8192], P('chan', 'seq'), may hold values from -6 to 6
- gate_two: bfloat16 [256, 8192], P('chan', 'seq'), may hold values from -6 to 6
- filter_one: float32 [256, 8192], P('chan', 'seq'), may hold values from -1 to 1
- filter_two: float32 [256, 8192], P('chan', 'seq'), may hold values from -1 to 1
- skip_one: float32 [256], P('chan'), may hold values from -1 to 1
- skip_two: float32 [256], P('chan'), may hold values from -1 to 1
- mix_weight: bfloat16 [256, 256], P(None, 'chan'), may hold values from -0.375 to 0.375
Outputs:
- mixed: bfloat16 [256, 8192], P('chan', 'seq')
The draws below stay inside these ranges and needn't reach their ends.
All inputs are finite; a program needn't handle non-finite values.
Results may differ from the reference program's by a relative error of at most 0.0051.
Values may be sent and summed in bfloat16 or wider, within the bound.
A program may use at most 64 MiB of HBM per device.

```python
import math
import jax
import jax.numpy as jnp
from jax import lax

D = 256
SEQ_LEN = 8192


def filter_law(key):
    streams = jax.random.split(key, 6)
    sequence_locations = jnp.arange(SEQ_LEN, dtype=jnp.float32)[None, :]
    fast_share = 0.4
    chooser = jax.random.uniform(streams[0], (D, 1))
    quick = jnp.exp(jax.random.uniform(streams[1], (D, 1), minval=math.log(10.0), maxval=math.log(40.0)))
    gentle = jnp.exp(jax.random.uniform(streams[2], (D, 1), minval=math.log(1.0 * SEQ_LEN), maxval=math.log(8.0 * SEQ_LEN)))
    lengths_of = jnp.where(chooser < fast_share, quick, gentle)
    nominal_dimensions = -sequence_locations / lengths_of
    destination_places = jax.random.randint(streams[3], (D, 4), 0, SEQ_LEN)
    discarded_elements = jnp.log(jax.random.uniform(streams[4], (D, 4), minval=0.5, maxval=0.8))
    for contiguous_group_number in range(4):
        following_update = sequence_locations >= destination_places[:, contiguous_group_number:contiguous_group_number + 1].astype(jnp.float32)
        nominal_dimensions = nominal_dimensions + discarded_elements[:, contiguous_group_number:contiguous_group_number + 1] * following_update.astype(jnp.float32)
    envelope = jnp.exp(nominal_dimensions)
    rough = jax.random.normal(streams[5], (D, SEQ_LEN))
    reshaped_rows = rough * envelope
    return reshaped_rows / jnp.sqrt(jnp.sum(reshaped_rows * reshaped_rows, axis=1, keepdims=True))


def draw_filter_one(key, part):
    return filter_law(jax.random.fold_in(key, 11)).astype(jnp.float32)


def draw_filter_two(key, part):
    return filter_law(jax.random.fold_in(key, 23)).astype(jnp.float32)


def block_levels(key, shape, cuts, low, high):
    def one(dim, shards_of):
        draws = jax.random.uniform(jax.random.fold_in(jax.random.fold_in(key, 6), dim), (shards_of,), jnp.float32, low / len(cuts), high / len(cuts))
        return jnp.repeat(jnp.exp(draws), shape[dim] // shards_of).reshape((-1,) + (1,) * (len(shape) - dim - 1))

    loudness = one(*cuts[0])
    for cut in cuts[1:]:
        loudness = loudness * one(*cut)
    return loudness


def normal_values(stream_key, dims, scale, reach, cuts=(), kind=jnp.bfloat16):
    factor_of = block_levels(stream_key, dims, cuts, -0.22, 0.18) if cuts else 1.0
    values = jax.random.normal(stream_key, dims, jnp.float32) * scale * factor_of
    return jnp.minimum(jnp.maximum(values, -reach), reach).astype(kind)


def setup_inputs(seed: int = 0) -> dict:
    arg_keys = jax.random.split(jax.random.key(seed), 9)
    values = normal_values(arg_keys[0], (D, SEQ_LEN), 1.0, 6.0, ((0, 2), (1, 16)))
    gate_one = normal_values(arg_keys[1], (D, SEQ_LEN), 1.0, 6.0, ((0, 2), (1, 16)))
    gate_two = normal_values(arg_keys[2], (D, SEQ_LEN), 1.0, 6.0, ((0, 2), (1, 16)))
    filter_one = draw_filter_one(jax.random.fold_in(arg_keys[8], 71), 0)
    filter_two = draw_filter_two(jax.random.fold_in(arg_keys[8], 71), 0)
    skip_one = jnp.clip(jax.random.uniform(arg_keys[5], (D,), jnp.float32, -1.0, 1.0) * block_levels(arg_keys[5], (D,), ((0, 2),), -0.4, 0.0), -1.0, 1.0)
    skip_two = jnp.clip(jax.random.uniform(arg_keys[6], (D,), jnp.float32, -1.0, 1.0) * block_levels(arg_keys[6], (D,), ((0, 2),), -0.4, 0.0), -1.0, 1.0)
    mix_weight = normal_values(arg_keys[7], (D, D), D ** -0.5, 0.375, ((1, 2),))
    return dict(values=values, gate_one=gate_one, gate_two=gate_two, filter_one=filter_one, filter_two=filter_two, skip_one=skip_one, skip_two=skip_two, mix_weight=mix_weight)


def causal(signal, filter_taps):
    padded = 2 * signal.shape[-1]
    spectrum = jnp.fft.rfft(signal, n=padded) * jnp.fft.rfft(filter_taps, n=padded)
    return jnp.fft.irfft(spectrum, n=padded)[..., :signal.shape[-1]].astype(jnp.float32)


def channel_block(pieces):
    values, gate_one, gate_two, filter_one, filter_two, skip_one, skip_two = pieces
    values_wide = values.astype(jnp.float32)
    conv_one = causal(values_wide, filter_one)
    gated = gate_one.astype(jnp.float32) * (conv_one + skip_one[:, None] * values_wide)
    conv_two = causal(gated, filter_two)
    return (gate_two.astype(jnp.float32) * (conv_two + skip_two[:, None] * gated)).astype(jnp.bfloat16)


def reference(values, gate_one, gate_two, filter_one, filter_two, skip_one, skip_two, mix_weight):
    blocks_of = 8

    def by_block(source):
        return source.reshape((D // blocks_of, blocks_of) + source.shape[1:])

    stacked = tuple(by_block(source) for source in (values, gate_one, gate_two, filter_one, filter_two, skip_one, skip_two))
    mixed_in = lax.map(channel_block, stacked).reshape(D, SEQ_LEN)
    summed = jnp.dot(mix_weight.T, mixed_in, preferred_element_type=jnp.float32)
    return jax.nn.silu(summed).astype(jnp.bfloat16)
```

```python
import functools

import jax
import jax.numpy as jnp
from jax import lax
from jax.experimental import pallas as pl
from jax.experimental.pallas import tpu as pltpu
from jax.sharding import PartitionSpec as P

LANES = 128
GROUP = 8


def toeplitz_conv(padded, taps, lags):
    row = lax.broadcasted_iota(jnp.int32, (LANES, LANES), 0)
    lane = lax.broadcasted_iota(jnp.int32, (LANES, LANES), 1)
    lower = lane >= row

    def step(group, carry):
        total, before = carry
        left, right = [], []
        for inner in range(GROUP):
            lag = group * GROUP + inner
            line = jnp.broadcast_to(taps[pl.ds(lag, 1), :], (LANES, LANES))
            turned = pltpu.roll(line, 0, 1, stride=1, stride_axis=0)
            right.append(jnp.where(lower, turned, before).astype(jnp.bfloat16))
            before = turned
            left.append(padded[pl.ds(lags - lag, lags), :].astype(jnp.bfloat16))
        total = total + jnp.dot(
            jnp.concatenate(left, axis=1),
            jnp.concatenate(right, axis=0),
            preferred_element_type=jnp.float32,
        )
        return total, before

    start = (jnp.zeros((lags, LANES), jnp.float32), jnp.zeros((LANES, LANES), jnp.float32))
    return lax.fori_loop(0, lags // GROUP, step, start)[0]


def conv_kernel(lags, values, gate, one, two, out, padded):
    padded[pl.ds(0, lags), :] = jnp.zeros((lags, LANES), jnp.float32)
    padded[pl.ds(lags, lags), :] = values[0].astype(jnp.float32)
    first = toeplitz_conv(padded, one.at[0], lags)
    padded[pl.ds(lags, lags), :] = gate[0].astype(jnp.float32) * first
    out[0] = toeplitz_conv(padded, two.at[0], lags).astype(out.dtype)


def both_convs(values, gate, one, two):
    count, lags, _ = values.shape
    block = pl.BlockSpec((1, lags, LANES), lambda c: (c, 0, 0))
    return pl.pallas_call(
        functools.partial(conv_kernel, lags),
        grid=(count,),
        in_specs=[block] * 4,
        out_specs=block,
        out_shape=jax.ShapeDtypeStruct(values.shape, jnp.bfloat16),
        scratch_shapes=[pltpu.VMEM((2 * lags, LANES), jnp.float32)],
    )(values, gate, one, two)


def per_device(seq, values, gate_one, gate_two, filter_one, filter_two, skip_one, skip_two, mix_weight):
    channels, tokens = values.shape
    each = -(-channels // seq)
    first_tap = (lax.iota(jnp.int32, tokens) == 0) & (lax.axis_index("seq") == 0)

    def with_skip(taps, skip):
        return (taps + jnp.where(first_tap[None, :], skip[:, None], 0.0)).astype(jnp.bfloat16)

    def spread(source):
        padded = jnp.pad(source, ((0, each * seq - channels), (0, 0)))
        return padded.reshape(seq, each, tokens)

    sent = jnp.stack(
        [
            spread(values),
            spread(gate_one),
            spread(with_skip(filter_one, skip_one)),
            spread(with_skip(filter_two, skip_two)),
        ],
        axis=1,
    )
    got = lax.all_to_all(sent, "seq", split_axis=0, concat_axis=0, tiled=True)
    lines = jnp.transpose(got, (1, 2, 0, 3)).reshape(4, each, seq * tokens // LANES, LANES)
    conv = both_convs(
        lines[0], lines[1], lines[2].astype(jnp.float32), lines[3].astype(jnp.float32)
    )
    back = jnp.transpose(conv.reshape(each, seq, tokens), (1, 0, 2))
    back = lax.all_to_all(back, "seq", split_axis=0, concat_axis=0, tiled=True)
    back = back.reshape(each * seq, tokens)[:channels]
    mixed_in = (gate_two.astype(jnp.float32) * back.astype(jnp.float32)).astype(jnp.bfloat16)
    summed = jnp.einsum(
        "de,dt->et",
        mix_weight,
        lax.all_gather(mixed_in, "chan", axis=0, tiled=True),
        preferred_element_type=jnp.float32,
    )
    return jax.nn.silu(summed).astype(jnp.bfloat16)


def solution(mesh):
    both = P("chan", "seq")
    return jax.shard_map(
        functools.partial(per_device, mesh.shape["seq"]),
        mesh=mesh,
        in_specs=(both, both, both, both, both, P("chan"), P("chan"), P(None, "chan")),
        out_specs=both,
        check_vma=False,
    )
```

```python
import functools
import math

import jax
import jax.numpy as jnp
from jax import lax
from jax.experimental import pallas as pl
from jax.experimental.pallas import tpu as pltpu
from jax.sharding import PartitionSpec as P

LANES = 128
GROUP = 64


def toeplitz_conv(padded, taps, lags, exact):
    group_size = math.gcd(lags, GROUP)
    row = lax.broadcasted_iota(jnp.int32, (LANES, LANES), 0)
    lane = lax.broadcasted_iota(jnp.int32, (LANES, LANES), 1)
    lower = lane >= row

    def step(group, carry):
        total, before = carry
        left, rest, right = [], [], []
        for inner in range(group_size):
            lag = group * group_size + inner
            line = jnp.broadcast_to(taps[pl.ds(lag, 1), :], (LANES, LANES))
            turned = pltpu.roll(line, 0, 1, stride=1, stride_axis=0)
            right.append(jnp.where(lower, turned, before).astype(jnp.bfloat16))
            before = turned
            moved = padded[pl.ds(lags - lag, lags), :]
            left.append(moved.astype(jnp.bfloat16))
            if not exact:
                rest.append((moved - left[-1].astype(jnp.float32)).astype(jnp.bfloat16))
        rows = [jnp.concatenate(left, axis=1)]
        if not exact:
            rows.append(jnp.concatenate(rest, axis=1))
        sums = jnp.dot(
            jnp.concatenate(rows, axis=0),
            jnp.concatenate(right, axis=0),
            preferred_element_type=jnp.float32,
        )
        total = total + sums[:lags]
        if not exact:
            total = total + sums[lags:]
        return total, before

    start = (jnp.zeros((lags, LANES), jnp.float32), jnp.zeros((LANES, LANES), jnp.float32))
    if group_size == lags:
        return step(0, start)[0]
    return lax.fori_loop(0, lags // group_size, step, start)[0]


def conv_kernel(lags, values, gate, gate_out, one, two, out, padded):
    padded[pl.ds(0, lags), :] = jnp.zeros((lags, LANES), jnp.float32)
    padded[pl.ds(lags, lags), :] = values[0].astype(jnp.float32)
    first = toeplitz_conv(padded, one.at[0], lags, True)
    padded[pl.ds(lags, lags), :] = gate[0].astype(jnp.float32) * first
    second = toeplitz_conv(padded, two.at[0], lags, True)
    out[0] = (gate_out[0].astype(jnp.float32) * second).astype(out.dtype)


def both_convs(values, gate, gate_out, one, two):
    count, lags, _ = values.shape
    block = pl.BlockSpec((1, lags, LANES), lambda c: (c, 0, 0))
    return pl.pallas_call(
        functools.partial(conv_kernel, lags),
        grid=(count,),
        in_specs=[block] * 5,
        out_specs=block,
        out_shape=jax.ShapeDtypeStruct(values.shape, jnp.bfloat16),
        scratch_shapes=[pltpu.VMEM((2 * lags, LANES), jnp.float32)],
    )(values, gate, gate_out, one, two)


def per_device(seq, values, gate_one, gate_two, filter_one, filter_two, skip_one, skip_two, mix_weight):
    channels, tokens = values.shape
    each = -(-channels // seq)
    first_tap = (lax.iota(jnp.int32, tokens) == 0) & (lax.axis_index("seq") == 0)

    def with_skip(taps, skip):
        return (taps + jnp.where(first_tap[None, :], skip[:, None], 0.0)).astype(jnp.bfloat16)

    def spread(source):
        padded = jnp.pad(source, ((0, each * seq - channels), (0, 0)))
        return padded.reshape(seq, each, tokens)

    sent = jnp.stack(
        [
            spread(values),
            spread(gate_one),
            spread(gate_two),
            spread(with_skip(filter_one, skip_one)),
            spread(with_skip(filter_two, skip_two)),
        ],
        axis=1,
    )
    got = lax.all_to_all(sent, "seq", split_axis=0, concat_axis=0, tiled=True)
    lines = jnp.transpose(got, (1, 2, 0, 3)).reshape(5, each, seq * tokens // LANES, LANES)
    conv = both_convs(
        lines[0], lines[1], lines[2], lines[3].astype(jnp.float32), lines[4].astype(jnp.float32)
    )
    back = jnp.transpose(conv.reshape(each, seq, tokens), (1, 0, 2))
    back = lax.all_to_all(back, "seq", split_axis=0, concat_axis=0, tiled=True)
    mixed_in = back.reshape(each * seq, tokens)[:channels]
    summed = jnp.einsum(
        "de,dt->et",
        mix_weight,
        lax.all_gather(mixed_in, "chan", axis=0, tiled=True),
        preferred_element_type=jnp.float32,
    )
    return jax.nn.silu(summed).astype(jnp.bfloat16)


def solution(mesh):
    both = P("chan", "seq")
    return jax.shard_map(
        functools.partial(per_device, mesh.shape["seq"]),
        mesh=mesh,
        in_specs=(both, both, both, both, both, P("chan"), P("chan"), P(None, "chan")),
        out_specs=both,
        check_vma=False,
    )
```

```python
import functools
import math

import jax
import jax.numpy as jnp
from jax import lax
from jax.experimental import pallas as pl
from jax.experimental.pallas import tpu as pltpu
from jax.sharding import PartitionSpec as P

LANES = 128
GROUP = 64
PARTS = 1
MESH = pl.DeviceIdType.MESH


def toeplitz_conv(padded, taps, lags):
    group_size = math.gcd(lags, GROUP)
    row = lax.broadcasted_iota(jnp.int32, (LANES, LANES), 0)
    lane = lax.broadcasted_iota(jnp.int32, (LANES, LANES), 1)
    lower = lane >= row

    def step(group, carry):
        total, before = carry
        left, right = [], []
        for inner in range(group_size):
            lag = group * group_size + inner
            line = jnp.broadcast_to(taps[pl.ds(lag, 1), :], (LANES, LANES))
            turned = pltpu.roll(line, 0, 1, stride=1, stride_axis=0)
            right.append(jnp.where(lower, turned, before).astype(jnp.bfloat16))
            before = turned
            left.append(padded[pl.ds(lags - lag, lags), :].astype(jnp.bfloat16))
        total = total + jnp.dot(
            jnp.concatenate(left, axis=1),
            jnp.concatenate(right, axis=0),
            preferred_element_type=jnp.float32,
        )
        return total, before

    start = (jnp.zeros((lags, LANES), jnp.float32), jnp.zeros((LANES, LANES), jnp.float32))
    if group_size == lags:
        return step(0, start)[0]
    return lax.fori_loop(0, lags // group_size, step, start)[0]


def rows_of(start, count, stride):
    return pl.ds(start, count, stride=stride) if count > 1 else pl.ds(start, 1)


def layer_kernel(
    seq, chan, each, parts, tokens,
    early, late, mix, out,
    got_early, got_late, lines, padded, ready, full, wide,
    early_out, early_in, late_out, late_in, back_out, back_in, pass_out, pass_in, own,
):
    me, mine = lax.axis_index("seq"), lax.axis_index("chan")
    tiles = tokens // LANES
    lags = seq * tiles
    share = each // parts

    def other(offset):
        return lax.rem(me + offset, seq)

    def sibling(offset):
        return lax.rem(mine + offset, chan)

    def to_peer(source, target, sent, landed, peer):
        return pltpu.make_async_remote_copy(
            src_ref=source, dst_ref=target, send_sem=sent, recv_sem=landed,
            device_id=(peer, mine), device_id_type=MESH,
        )

    def early_copy(peer, slot):
        return to_peer(early.at[peer], got_early.at[slot], early_out.at[peer], early_in.at[slot], peer)

    def late_copy(peer, slot):
        return to_peer(late.at[peer], got_late.at[slot], late_out.at[peer], late_in.at[slot], peer)

    def back_copy(part, peer, slot):
        return to_peer(
            ready.at[part, peer], full.at[mine, slot, part],
            back_out.at[part, peer], back_in.at[part, slot], peer,
        )

    def pass_copy(part, slot, group, offset):
        return pltpu.make_async_remote_copy(
            src_ref=full.at[group, slot, part], dst_ref=full.at[group, slot, part],
            send_sem=pass_out.at[part, offset, slot], recv_sem=pass_in.at[part, group, slot],
            device_id=(me, sibling(offset)), device_id_type=MESH,
        )

    def each_other(body):
        def step(offset, carry):
            body(other(offset))
            return carry

        lax.fori_loop(1, seq, step, 0)

    barrier = pltpu.get_barrier_semaphore()
    each_other(
        lambda peer: pl.semaphore_signal(barrier, inc=1, device_id=(peer, mine), device_id_type=MESH)
    )
    for offset in range(1, chan):
        pl.semaphore_signal(barrier, inc=1, device_id=(me, sibling(offset)), device_id_type=MESH)
    pl.semaphore_wait(barrier, seq - 1 + chan - 1)

    each_other(lambda peer: early_copy(peer, me).start())
    each_other(lambda peer: late_copy(peer, me).start())
    own_early = pltpu.make_async_copy(early.at[me], got_early.at[me], own.at[0])
    own_late = pltpu.make_async_copy(late.at[me], got_late.at[me], own.at[1])
    own_early.start()
    own_late.start()
    padded[pl.ds(0, lags), :] = jnp.zeros((lags, LANES), jnp.float32)

    def lay_out(got, piece, first):
        def step(source, carry):
            for index in range(got.shape[1]):
                block = got[source, index].astype(jnp.float32)
                for tile in range(tiles):
                    lines[first + index, rows_of(source * tiles + tile, each, lags), :] = block[
                        :, tile * LANES : (tile + 1) * LANES
                    ]
            return carry

        lax.fori_loop(0, seq, step, 0)

    each_other(lambda peer: early_copy(peer, peer).wait_recv())
    own_early.wait()
    lay_out(got_early, 2, 0)

    def first_conv(channel, carry):
        base = pl.multiple_of(channel * lags, lags)
        padded[pl.ds(lags, lags), :] = lines[0, pl.ds(base, lags), :]
        lines[0, pl.ds(base, lags), :] = toeplitz_conv(padded, lines.at[1, pl.ds(base, lags)], lags)
        return carry

    lax.fori_loop(0, each, first_conv, 0)

    each_other(lambda peer: late_copy(peer, peer).wait_recv())
    own_late.wait()
    lay_out(got_late, 3, 2)

    def second_conv(channel, carry):
        base = pl.multiple_of(channel * lags, lags)
        here = pl.ds(base, lags)
        padded[pl.ds(lags, lags), :] = lines[2, here, :] * lines[0, here, :]
        second = toeplitz_conv(padded, lines.at[4, here], lags)
        lines[0, here, :] = lines[3, here, :] * second
        return carry

    own_back = []
    for part in range(parts):
        lax.fori_loop(part * share, (part + 1) * share, second_conv, 0)

        def gather(target, carry, part=part):
            for tile in range(tiles):
                ready[part, target, :, pl.ds(tile * LANES, LANES)] = lines[
                    0, rows_of(part * share * lags + target * tiles + tile, share, lags), :
                ].astype(ready.dtype)
            return carry

        lax.fori_loop(0, seq, gather, 0)
        each_other(lambda peer, part=part: back_copy(part, peer, me).start())
        own_back.append(
            pltpu.make_async_copy(ready.at[part, me], full.at[mine, me, part], own.at[2 + part])
        )
        own_back[-1].start()

    def pass_on(part, slot):
        for offset in range(1, chan):
            pass_copy(part, slot, mine, offset).start()

    for part in range(parts):
        own_back[part].wait()
        pass_on(part, me)

        def arrived(peer, part=part):
            back_copy(part, peer, peer).wait_recv()
            pass_on(part, peer)

        each_other(arrived)

    def widen(group, slot):
        for part in range(parts):
            wide[pl.ds((group * seq + slot) * each + part * share, share), :] = full[
                group, slot, part
            ].astype(jnp.float32)

    def widen_mine(slot, carry):
        widen(mine, slot)
        return carry

    lax.fori_loop(0, seq, widen_mine, 0)
    for offset in range(1, chan):
        group = sibling(offset)

        def widen_other(slot, carry, group=group, offset=offset):
            for part in range(parts):
                pass_copy(part, slot, group, offset).wait_recv()
            widen(group, slot)
            return carry

        lax.fori_loop(0, seq, widen_other, 0)

    summed = jnp.dot(mix[...], wide[...].astype(jnp.bfloat16), preferred_element_type=jnp.float32)
    out[...] = (summed / (1.0 + jnp.exp(-summed))).astype(out.dtype)

    each_other(lambda peer: early_copy(peer, me).wait_send())
    each_other(lambda peer: late_copy(peer, me).wait_send())
    for part in range(parts):
        each_other(lambda peer, part=part: back_copy(part, peer, me).wait_send())
        for offset in range(1, chan):

            def sent(slot, carry, part=part, offset=offset):
                pass_copy(part, slot, mine, offset).wait_send()
                return carry

            lax.fori_loop(0, seq, sent, 0)


def per_device(
    seq, chan, values, gate_one, gate_two, filter_one, filter_two, skip_one, skip_two, mix_weight
):
    channels, tokens = values.shape
    made = mix_weight.shape[1]
    each = -(-channels // seq)
    parts = math.gcd(each, PARTS)
    lags = seq * tokens // LANES
    room = each * seq
    first_tap = (lax.iota(jnp.int32, tokens) == 0) & (lax.axis_index("seq") == 0)

    def with_skip(taps, skip):
        return (taps + jnp.where(first_tap[None, :], skip[:, None], 0.0)).astype(jnp.bfloat16)

    def spread(*sources):
        return jnp.stack(
            [
                jnp.pad(source, ((0, room - channels), (0, 0))).reshape(seq, each, tokens)
                for source in sources
            ],
            axis=1,
        )

    early = spread(values, with_skip(filter_one, skip_one))
    late = spread(gate_one, gate_two, with_skip(filter_two, skip_two))
    mix = jnp.pad(
        mix_weight.T.reshape(made, chan, channels), ((0, 0), (0, 0), (0, room - channels))
    ).reshape(made, chan * room)
    anywhere = pl.BlockSpec(memory_space=pl.ANY)
    vmem = pl.BlockSpec(memory_space=pltpu.VMEM)
    dma = pltpu.SemaphoreType.DMA
    share = each // parts
    return pl.pallas_call(
        functools.partial(layer_kernel, seq, chan, each, parts, tokens),
        in_specs=[anywhere, anywhere, vmem],
        out_specs=vmem,
        out_shape=jax.ShapeDtypeStruct((made, tokens), jnp.bfloat16),
        scratch_shapes=[
            pltpu.VMEM((seq, 2, each, tokens), jnp.bfloat16),
            pltpu.VMEM((seq, 3, each, tokens), jnp.bfloat16),
            pltpu.VMEM((5, each * lags, LANES), jnp.float32),
            pltpu.VMEM((2 * lags, LANES), jnp.float32),
            pltpu.VMEM((parts, seq, share, tokens), jnp.bfloat16),
            pltpu.VMEM((chan, seq, parts, share, tokens), jnp.bfloat16),
            pltpu.VMEM((chan * room, tokens), jnp.float32),
            dma((seq,)),
            dma((seq,)),
            dma((seq,)),
            dma((seq,)),
            dma((parts, seq)),
            dma((parts, seq)),
            dma((parts, chan, seq)),
            dma((parts, chan, seq)),
            dma((2 + parts,)),
        ],
        compiler_params=pltpu.CompilerParams(collective_id=0, has_side_effects=True),
    )(early, late, mix)


def solution(mesh):
    both = P("chan", "seq")
    return jax.shard_map(
        functools.partial(per_device, mesh.shape["seq"], mesh.shape["chan"]),
        mesh=mesh,
        in_specs=(both, both, both, both, both, P("chan"), P("chan"), P(None, "chan")),
        out_specs=both,
        check_vma=False,
    )
```

```python
import functools
import math

import jax
import jax.numpy as jnp
from jax import lax
from jax.experimental import pallas as pl
from jax.experimental.pallas import tpu as pltpu
from jax.sharding import PartitionSpec as P

LANES = 128
GROUP = 64
PARTS = 1
MESH = pl.DeviceIdType.MESH


def toeplitz_conv(padded, taps, lags):
    group_size = math.gcd(lags, GROUP)
    row = lax.broadcasted_iota(jnp.int32, (LANES, LANES), 0)
    lane = lax.broadcasted_iota(jnp.int32, (LANES, LANES), 1)
    lower = lane >= row

    def step(group, carry):
        total, before = carry
        left, right = [], []
        for inner in range(group_size):
            lag = group * group_size + inner
            line = jnp.broadcast_to(taps[pl.ds(lag, 1), :], (LANES, LANES))
            turned = pltpu.roll(line, 0, 1, stride=1, stride_axis=0)
            right.append(jnp.where(lower, turned, before).astype(jnp.bfloat16))
            before = turned
            left.append(padded[pl.ds(lags - lag, lags), :].astype(jnp.bfloat16))
        total = total + jnp.dot(
            jnp.concatenate(left, axis=1),
            jnp.concatenate(right, axis=0),
            preferred_element_type=jnp.float32,
        )
        return total, before

    start = (jnp.zeros((lags, LANES), jnp.float32), jnp.zeros((LANES, LANES), jnp.float32))
    if group_size == lags:
        return step(0, start)[0]
    return lax.fori_loop(0, lags // group_size, step, start)[0]


def rows_of(start, count, stride):
    return pl.ds(start, count, stride=stride) if count > 1 else pl.ds(start, 1)


def layer_kernel(
    seq, chan, each, parts, tokens,
    values, gate_one, gate_two, filter_one, filter_two, skip_one, skip_two, mix, out,
    taps_one, taps_two, direct, got, lines, padded, ready, full, wide,
    sent_out, sent_in, back_out, back_in, pass_out, pass_in, own,
):
    me, mine = lax.axis_index("seq"), lax.axis_index("chan")
    tiles = tokens // LANES
    lags = seq * tiles
    share = each // parts

    def other(offset):
        return lax.rem(me + offset, seq)

    def sibling(offset):
        return lax.rem(mine + offset, chan)

    def to_peer(source, target, sent, landed, peer):
        return pltpu.make_async_remote_copy(
            src_ref=source, dst_ref=target, send_sem=sent, recv_sem=landed,
            device_id=(peer, mine), device_id_type=MESH,
        )

    pieces = (values, taps_one, gate_one, taps_two, gate_two)
    early, late = (0, 1), (2, 3, 4)

    def piece_copy(piece, peer, slot):
        return to_peer(
            pieces[piece].at[peer], got.at[piece, slot],
            sent_out.at[piece, peer], sent_in.at[piece, slot], peer,
        )

    def back_copy(part, peer, slot):
        return to_peer(
            ready.at[part, peer], full.at[mine, slot, part],
            back_out.at[part, peer], back_in.at[part, slot], peer,
        )

    def pass_copy(part, slot, group, offset):
        return pltpu.make_async_remote_copy(
            src_ref=full.at[group, slot, part], dst_ref=full.at[group, slot, part],
            send_sem=pass_out.at[part, offset, slot], recv_sem=pass_in.at[part, group, slot],
            device_id=(me, sibling(offset)), device_id_type=MESH,
        )

    def each_other(body):
        def step(offset, carry):
            body(other(offset))
            return carry

        lax.fori_loop(1, seq, step, 0)

    barrier = pltpu.get_barrier_semaphore()
    each_other(
        lambda peer: pl.semaphore_signal(barrier, inc=1, device_id=(peer, mine), device_id_type=MESH)
    )
    for offset in range(1, chan):
        pl.semaphore_signal(barrier, inc=1, device_id=(me, sibling(offset)), device_id_type=MESH)
    room = seq * each
    for taps, source, skip in ((taps_one, filter_one, skip_one), (taps_two, filter_two, skip_two)):
        row = lax.broadcasted_iota(jnp.int32, (room, room), 0)
        lane = lax.broadcasted_iota(jnp.int32, (room, room), 1)
        column = jnp.sum(
            jnp.where(row == lane, jnp.broadcast_to(skip[...], (room, room)), 0.0), axis=1, keepdims=True
        )
        lane = lax.broadcasted_iota(jnp.int32, (room, LANES), 1)
        direct[...] = jnp.where(lane + me == 0, column, 0.0)

        def make_taps(target, carry, taps=taps, source=source):
            for tile in range(tiles):
                part = source[target, :, pl.ds(tile * LANES, LANES)]
                if tile == 0:
                    part = part + direct[pl.ds(target * each, each), :]
                taps[target, :, pl.ds(tile * LANES, LANES)] = part.astype(taps.dtype)
            return carry

        lax.fori_loop(0, seq, make_taps, 0)
    pl.semaphore_wait(barrier, seq - 1 + chan - 1)

    own_copies = [
        pltpu.make_async_copy(pieces[piece].at[me], got.at[piece, me], own.at[piece])
        for piece in early + late
    ]
    for group in (early, late):

        def send(peer, group=group):
            for piece in group:
                piece_copy(piece, peer, me).start()

        each_other(send)
        for piece in group:
            own_copies[piece].start()
    padded[pl.ds(0, lags), :] = jnp.zeros((lags, LANES), jnp.float32)

    def lay_out(group):
        def wait(peer):
            for piece in group:
                piece_copy(piece, peer, peer).wait_recv()

        each_other(wait)
        for piece in group:
            own_copies[piece].wait()

        def step(source, carry):
            for piece in group:
                block = got[piece, source].astype(jnp.float32)
                for tile in range(tiles):
                    lines[piece, rows_of(source * tiles + tile, each, lags), :] = block[
                        :, tile * LANES : (tile + 1) * LANES
                    ]
            return carry

        lax.fori_loop(0, seq, step, 0)

    lay_out(early)

    def first_conv(channel, carry):
        base = pl.multiple_of(channel * lags, lags)
        padded[pl.ds(lags, lags), :] = lines[0, pl.ds(base, lags), :]
        lines[0, pl.ds(base, lags), :] = toeplitz_conv(padded, lines.at[1, pl.ds(base, lags)], lags)
        return carry

    lax.fori_loop(0, each, first_conv, 0)

    lay_out(late)

    def second_conv(channel, carry):
        base = pl.multiple_of(channel * lags, lags)
        here = pl.ds(base, lags)
        padded[pl.ds(lags, lags), :] = lines[2, here, :] * lines[0, here, :]
        second = toeplitz_conv(padded, lines.at[3, here], lags)
        lines[0, here, :] = lines[4, here, :] * second
        return carry

    own_back = []
    for part in range(parts):
        lax.fori_loop(part * share, (part + 1) * share, second_conv, 0)

        def gather(target, carry, part=part):
            for tile in range(tiles):
                ready[part, target, :, pl.ds(tile * LANES, LANES)] = lines[
                    0, rows_of(part * share * lags + target * tiles + tile, share, lags), :
                ].astype(ready.dtype)
            return carry

        lax.fori_loop(0, seq, gather, 0)
        each_other(lambda peer, part=part: back_copy(part, peer, me).start())
        own_back.append(
            pltpu.make_async_copy(ready.at[part, me], full.at[mine, me, part], own.at[len(pieces) + part])
        )
        own_back[-1].start()

    def pass_on(part, slot):
        for offset in range(1, chan):
            pass_copy(part, slot, mine, offset).start()

    for part in range(parts):
        own_back[part].wait()
        pass_on(part, me)

        def arrived(peer, part=part):
            back_copy(part, peer, peer).wait_recv()
            pass_on(part, peer)

        each_other(arrived)

    def widen(group, slot):
        for part in range(parts):
            wide[pl.ds((group * seq + slot) * each + part * share, share), :] = full[
                group, slot, part
            ].astype(jnp.float32)

    def widen_mine(slot, carry):
        widen(mine, slot)
        return carry

    lax.fori_loop(0, seq, widen_mine, 0)
    for offset in range(1, chan):
        group = sibling(offset)

        def widen_other(slot, carry, group=group, offset=offset):
            for part in range(parts):
                pass_copy(part, slot, group, offset).wait_recv()
            widen(group, slot)
            return carry

        lax.fori_loop(0, seq, widen_other, 0)

    out[...] = lax.dot_general(
        mix[...],
        wide[...].astype(jnp.bfloat16),
        (((0,), (0,)), ((), ())),
        preferred_element_type=jnp.float32,
    )

    for piece in early + late:
        each_other(lambda peer, piece=piece: piece_copy(piece, peer, me).wait_send())
    for part in range(parts):
        each_other(lambda peer, part=part: back_copy(part, peer, me).wait_send())
        for offset in range(1, chan):

            def sent(slot, carry, part=part, offset=offset):
                pass_copy(part, slot, mine, offset).wait_send()
                return carry

            lax.fori_loop(0, seq, sent, 0)


def per_device(
    seq, chan, values, gate_one, gate_two, filter_one, filter_two, skip_one, skip_two, mix_weight
):
    channels, tokens = values.shape
    made = mix_weight.shape[1]
    each = -(-channels // seq)
    parts = math.gcd(each, PARTS)
    lags = seq * tokens // LANES
    room = each * seq

    def spread(source):
        return jnp.pad(source, ((0, room - channels), (0, 0))).reshape(seq, each, tokens)

    def lane_row(skip):
        return jnp.pad(skip, (0, room - channels)).reshape(1, room)

    mix = jnp.pad(
        mix_weight.reshape(chan, channels, made), ((0, 0), (0, room - channels), (0, 0))
    ).reshape(chan * room, made)
    anywhere = pl.BlockSpec(memory_space=pl.ANY)
    vmem = pl.BlockSpec(memory_space=pltpu.VMEM)
    dma = pltpu.SemaphoreType.DMA
    share = each // parts
    summed = pl.pallas_call(
        functools.partial(layer_kernel, seq, chan, each, parts, tokens),
        in_specs=[anywhere] * 3 + [vmem] * 5,
        out_specs=vmem,
        out_shape=jax.ShapeDtypeStruct((made, tokens), jnp.float32),
        scratch_shapes=[
            pltpu.VMEM((seq, each, tokens), jnp.bfloat16),
            pltpu.VMEM((seq, each, tokens), jnp.bfloat16),
            pltpu.VMEM((room, LANES), jnp.float32),
            pltpu.VMEM((5, seq, each, tokens), jnp.bfloat16),
            pltpu.VMEM((5, each * lags, LANES), jnp.float32),
            pltpu.VMEM((2 * lags, LANES), jnp.float32),
            pltpu.VMEM((parts, seq, share, tokens), jnp.bfloat16),
            pltpu.VMEM((chan, seq, parts, share, tokens), jnp.bfloat16),
            pltpu.VMEM((chan * room, tokens), jnp.float32),
            dma((5, seq)),
            dma((5, seq)),
            dma((parts, seq)),
            dma((parts, seq)),
            dma((parts, chan, seq)),
            dma((parts, chan, seq)),
            dma((5 + parts,)),
        ],
        compiler_params=pltpu.CompilerParams(collective_id=0, has_side_effects=True),
    )(
        spread(values), spread(gate_one), spread(gate_two), spread(filter_one), spread(filter_two),
        lane_row(skip_one), lane_row(skip_two), mix,
    )
    return (summed / (1.0 + jnp.exp(-summed))).astype(jnp.bfloat16)


def solution(mesh):
    both = P("chan", "seq")
    return jax.shard_map(
        functools.partial(per_device, mesh.shape["seq"], mesh.shape["chan"]),
        mesh=mesh,
        in_specs=(both, both, both, both, both, P("chan"), P("chan"), P(None, "chan")),
        out_specs=both,
        check_vma=False,
    )
```

```python
import functools
import math

import jax
import jax.numpy as jnp
from jax import lax
from jax.experimental import pallas as pl
from jax.experimental.pallas import tpu as pltpu
from jax.sharding import PartitionSpec as P

LANES = 128
GROUP = 64
PARTS = 2
MESH = pl.DeviceIdType.MESH


def toeplitz_conv(padded, taps, lags):
    group_size = math.gcd(lags, GROUP)
    row = lax.broadcasted_iota(jnp.int32, (LANES, LANES), 0)
    lane = lax.broadcasted_iota(jnp.int32, (LANES, LANES), 1)
    lower = lane >= row

    def step(group, carry):
        total, before = carry
        left, right = [], []
        for inner in range(group_size):
            lag = group * group_size + inner
            line = jnp.broadcast_to(taps[pl.ds(lag, 1), :], (LANES, LANES))
            turned = pltpu.roll(line, 0, 1, stride=1, stride_axis=0)
            right.append(jnp.where(lower, turned, before).astype(jnp.bfloat16))
            before = turned
            left.append(padded[pl.ds(lags - lag, lags), :].astype(jnp.bfloat16))
        total = total + jnp.dot(
            jnp.concatenate(left, axis=1),
            jnp.concatenate(right, axis=0),
            preferred_element_type=jnp.float32,
        )
        return total, before

    start = (jnp.zeros((lags, LANES), jnp.float32), jnp.zeros((LANES, LANES), jnp.float32))
    if group_size == lags:
        return step(0, start)[0]
    return lax.fori_loop(0, lags // group_size, step, start)[0]


def rows_of(start, count, stride):
    return pl.ds(start, count, stride=stride) if count > 1 else pl.ds(start, 1)


def layer_kernel(
    seq, chan, each, parts, tokens,
    values, gate_one, gate_two, filter_one, filter_two, skip_one, skip_two, mix, out,
    taps_one, taps_two, direct, got, lines, padded, ready, full, wide,
    sent_out, sent_in, back_out, back_in, pass_out, pass_in, own,
):
    me, mine = lax.axis_index("seq"), lax.axis_index("chan")
    tiles = tokens // LANES
    lags = seq * tiles
    share = each // parts

    def other(offset):
        return lax.rem(me + offset, seq)

    def sibling(offset):
        return lax.rem(mine + offset, chan)

    def to_peer(source, target, sent, landed, peer):
        return pltpu.make_async_remote_copy(
            src_ref=source, dst_ref=target, send_sem=sent, recv_sem=landed,
            device_id=(peer, mine), device_id_type=MESH,
        )

    pieces = (values, taps_one, gate_one, taps_two, gate_two)
    early, late = (0, 1), (2, 3, 4)

    def rows(part):
        return pl.ds(part * share, share)

    def piece_copy(part, piece, peer, slot):
        return to_peer(
            pieces[piece].at[peer, rows(part)], got.at[piece, slot, rows(part)],
            sent_out.at[part, piece, peer], sent_in.at[part, piece, slot], peer,
        )

    def back_copy(part, peer, slot):
        return to_peer(
            ready.at[peer, rows(part)], full.at[mine, slot, rows(part)],
            back_out.at[part, peer], back_in.at[part, slot], peer,
        )

    def pass_copy(part, slot, group, offset):
        return pltpu.make_async_remote_copy(
            src_ref=full.at[group, slot, rows(part)], dst_ref=full.at[group, slot, rows(part)],
            send_sem=pass_out.at[part, offset, slot], recv_sem=pass_in.at[part, group, slot],
            device_id=(me, sibling(offset)), device_id_type=MESH,
        )

    def each_other(body):
        def step(offset, carry):
            body(other(offset))
            return carry

        lax.fori_loop(1, seq, step, 0)

    barrier = pltpu.get_barrier_semaphore()
    each_other(
        lambda peer: pl.semaphore_signal(barrier, inc=1, device_id=(peer, mine), device_id_type=MESH)
    )
    for offset in range(1, chan):
        pl.semaphore_signal(barrier, inc=1, device_id=(me, sibling(offset)), device_id_type=MESH)
    room = seq * each
    for taps, source, skip in ((taps_one, filter_one, skip_one), (taps_two, filter_two, skip_two)):
        row = lax.broadcasted_iota(jnp.int32, (room, room), 0)
        lane = lax.broadcasted_iota(jnp.int32, (room, room), 1)
        column = jnp.sum(
            jnp.where(row == lane, jnp.broadcast_to(skip[...], (room, room)), 0.0), axis=1, keepdims=True
        )
        lane = lax.broadcasted_iota(jnp.int32, (room, LANES), 1)
        direct[...] = jnp.where(lane + me == 0, column, 0.0)

        def make_taps(target, carry, taps=taps, source=source):
            for tile in range(tiles):
                part = source[target, :, pl.ds(tile * LANES, LANES)]
                if tile == 0:
                    part = part + direct[pl.ds(target * each, each), :]
                taps[target, :, pl.ds(tile * LANES, LANES)] = part.astype(taps.dtype)
            return carry

        lax.fori_loop(0, seq, make_taps, 0)
    pl.semaphore_wait(barrier, seq - 1 + chan - 1)

    own_copies = [
        pltpu.make_async_copy(pieces[piece].at[me], got.at[piece, me], own.at[piece])
        for piece in early + late
    ]
    for group in (early, late):
        for part in range(parts):

            def send(peer, group=group, part=part):
                for piece in group:
                    piece_copy(part, piece, peer, me).start()

            each_other(send)
            if part == 0:
                for piece in group:
                    own_copies[piece].start()
    padded[pl.ds(0, lags), :] = jnp.zeros((lags, LANES), jnp.float32)

    def lay_out(group, part):
        def wait(peer):
            for piece in group:
                piece_copy(part, piece, peer, peer).wait_recv()

        each_other(wait)
        if part == 0:
            for piece in group:
                own_copies[piece].wait()

        def step(source, carry):
            for piece in group:
                for tile in range(tiles):
                    block = got[piece, source, rows(part), pl.ds(tile * LANES, LANES)]
                    lines[
                        piece, rows_of(part * share * lags + source * tiles + tile, share, lags), :
                    ] = block.astype(jnp.float32)
            return carry

        lax.fori_loop(0, seq, step, 0)

    def first_conv(channel, carry):
        base = pl.multiple_of(channel * lags, lags)
        padded[pl.ds(lags, lags), :] = lines[0, pl.ds(base, lags), :]
        lines[0, pl.ds(base, lags), :] = toeplitz_conv(padded, lines.at[1, pl.ds(base, lags)], lags)
        return carry

    for part in range(parts):
        lay_out(early, part)
        lax.fori_loop(part * share, (part + 1) * share, first_conv, 0)

    def second_conv(channel, carry):
        base = pl.multiple_of(channel * lags, lags)
        here = pl.ds(base, lags)
        padded[pl.ds(lags, lags), :] = lines[2, here, :] * lines[0, here, :]
        second = toeplitz_conv(padded, lines.at[3, here], lags)
        lines[0, here, :] = lines[4, here, :] * second
        return carry

    own_back = []
    for part in range(parts):
        lay_out(late, part)
        lax.fori_loop(part * share, (part + 1) * share, second_conv, 0)

        def gather(target, carry, part=part):
            for tile in range(tiles):
                ready[target, rows(part), pl.ds(tile * LANES, LANES)] = lines[
                    0, rows_of(part * share * lags + target * tiles + tile, share, lags), :
                ].astype(ready.dtype)
            return carry

        lax.fori_loop(0, seq, gather, 0)
        each_other(lambda peer, part=part: back_copy(part, peer, me).start())
        own_back.append(
            pltpu.make_async_copy(
                ready.at[me, rows(part)], full.at[mine, me, rows(part)], own.at[len(pieces) + part]
            )
        )
        own_back[-1].start()

    def pass_on(part, slot):
        for offset in range(1, chan):
            pass_copy(part, slot, mine, offset).start()

    for part in range(parts):
        own_back[part].wait()
        pass_on(part, me)

        def arrived(peer, part=part):
            back_copy(part, peer, peer).wait_recv()
            pass_on(part, peer)

        each_other(arrived)

    def widen(group, slot):
        wide[pl.ds((group * seq + slot) * each, each), :] = full[group, slot].astype(jnp.float32)

    def widen_mine(slot, carry):
        widen(mine, slot)
        return carry

    lax.fori_loop(0, seq, widen_mine, 0)
    for offset in range(1, chan):
        group = sibling(offset)

        def widen_other(slot, carry, group=group, offset=offset):
            for part in range(parts):
                pass_copy(part, slot, group, offset).wait_recv()
            widen(group, slot)
            return carry

        lax.fori_loop(0, seq, widen_other, 0)

    out[...] = lax.dot_general(
        mix[...],
        wide[...].astype(jnp.bfloat16),
        (((0,), (0,)), ((), ())),
        preferred_element_type=jnp.float32,
    )

    for part in range(parts):
        for piece in early + late:
            each_other(
                lambda peer, piece=piece, part=part: piece_copy(part, piece, peer, me).wait_send()
            )
        each_other(lambda peer, part=part: back_copy(part, peer, me).wait_send())
        for offset in range(1, chan):

            def sent(slot, carry, part=part, offset=offset):
                pass_copy(part, slot, mine, offset).wait_send()
                return carry

            lax.fori_loop(0, seq, sent, 0)


def per_device(
    seq, chan, values, gate_one, gate_two, filter_one, filter_two, skip_one, skip_two, mix_weight
):
    channels, tokens = values.shape
    made = mix_weight.shape[1]
    each = -(-channels // seq)
    parts = math.gcd(each, PARTS)
    lags = seq * tokens // LANES
    room = each * seq

    def spread(source):
        return jnp.pad(source, ((0, room - channels), (0, 0))).reshape(seq, each, tokens)

    def lane_row(skip):
        return jnp.pad(skip, (0, room - channels)).reshape(1, room)

    mix = jnp.pad(
        mix_weight.reshape(chan, channels, made), ((0, 0), (0, room - channels), (0, 0))
    ).reshape(chan * room, made)
    anywhere = pl.BlockSpec(memory_space=pl.ANY)
    vmem = pl.BlockSpec(memory_space=pltpu.VMEM)
    dma = pltpu.SemaphoreType.DMA
    summed = pl.pallas_call(
        functools.partial(layer_kernel, seq, chan, each, parts, tokens),
        in_specs=[anywhere] * 3 + [vmem] * 5,
        out_specs=vmem,
        out_shape=jax.ShapeDtypeStruct((made, tokens), jnp.float32),
        scratch_shapes=[
            pltpu.VMEM((seq, each, tokens), jnp.bfloat16),
            pltpu.VMEM((seq, each, tokens), jnp.bfloat16),
            pltpu.VMEM((room, LANES), jnp.float32),
            pltpu.VMEM((5, seq, each, tokens), jnp.bfloat16),
            pltpu.VMEM((5, each * lags, LANES), jnp.float32),
            pltpu.VMEM((2 * lags, LANES), jnp.float32),
            pltpu.VMEM((seq, each, tokens), jnp.bfloat16),
            pltpu.VMEM((chan, seq, each, tokens), jnp.bfloat16),
            pltpu.VMEM((chan * room, tokens), jnp.float32),
            dma((parts, 5, seq)),
            dma((parts, 5, seq)),
            dma((parts, seq)),
            dma((parts, seq)),
            dma((parts, chan, seq)),
            dma((parts, chan, seq)),
            dma((5 + parts,)),
        ],
        compiler_params=pltpu.CompilerParams(collective_id=0, has_side_effects=True),
    )(
        spread(values), spread(gate_one), spread(gate_two), spread(filter_one), spread(filter_two),
        lane_row(skip_one), lane_row(skip_two), mix,
    )
    return (summed / (1.0 + jnp.exp(-summed))).astype(jnp.bfloat16)


def solution(mesh):
    both = P("chan", "seq")
    return jax.shard_map(
        functools.partial(per_device, mesh.shape["seq"], mesh.shape["chan"]),
        mesh=mesh,
        in_specs=(both, both, both, both, both, P("chan"), P("chan"), P(None, "chan")),
        out_specs=both,
        check_vma=False,
    )
```

```python
import functools
import math

import jax
import jax.numpy as jnp
from jax import lax
from jax.experimental import pallas as pl
from jax.experimental.pallas import tpu as pltpu
from jax.sharding import PartitionSpec as P

LANES = 128
GROUP = 64
PARTS = 1
MESH = pl.DeviceIdType.MESH


def toeplitz_conv(padded, taps, lags):
    group_size = math.gcd(lags, GROUP)
    row = lax.broadcasted_iota(jnp.int32, (LANES, LANES), 0)
    lane = lax.broadcasted_iota(jnp.int32, (LANES, LANES), 1)
    lower = lane >= row

    def step(group, carry):
        total, before = carry
        left, right = [], []
        for inner in range(group_size):
            lag = group * group_size + inner
            line = jnp.broadcast_to(taps[pl.ds(lag, 1), :], (LANES, LANES))
            turned = pltpu.roll(line, 0, 1, stride=1, stride_axis=0)
            right.append(jnp.where(lower, turned, before).astype(jnp.bfloat16))
            before = turned
            left.append(padded[pl.ds(lags - lag, lags), :].astype(jnp.bfloat16))
        total = total + jnp.dot(
            jnp.concatenate(left, axis=1),
            jnp.concatenate(right, axis=0),
            preferred_element_type=jnp.float32,
        )
        return total, before

    start = (jnp.zeros((lags, LANES), jnp.float32), jnp.zeros((LANES, LANES), jnp.float32))
    if group_size == lags:
        return step(0, start)[0]
    return lax.fori_loop(0, lags // group_size, step, start)[0]


def rows_of(start, count, stride):
    return pl.ds(start, count, stride=stride) if count > 1 else pl.ds(start, 1)


def layer_kernel(
    seq, chan, each, parts, tokens,
    values, gate_one, gate_two, filter_one, filter_two, skip_one, skip_two, mix, out,
    boxes_early, boxes_late, got_early, got_late, direct, lines, padded, ready, full, wide,
    sent_out, sent_in, back_out, back_in, pass_out, pass_in, own,
):
    me, mine = lax.axis_index("seq"), lax.axis_index("chan")
    tiles = tokens // LANES
    lags = seq * tiles
    share = each // parts

    def other(offset):
        return lax.rem(me + offset, seq)

    def sibling(offset):
        return lax.rem(mine + offset, chan)

    def to_peer(source, target, sent, landed, peer):
        return pltpu.make_async_remote_copy(
            src_ref=source, dst_ref=target, send_sem=sent, recv_sem=landed,
            device_id=(peer, mine), device_id_type=MESH,
        )

    boxes, got = (boxes_early, boxes_late), (got_early, got_late)

    def rows(part):
        return pl.ds(part * share, share)

    def box_copy(group, peer, slot):
        return to_peer(
            boxes[group].at[peer], got[group].at[slot],
            sent_out.at[group, peer], sent_in.at[group, slot], peer,
        )

    def back_copy(part, peer, slot):
        return to_peer(
            ready.at[peer, rows(part)], full.at[mine, slot, rows(part)],
            back_out.at[part, peer], back_in.at[part, slot], peer,
        )

    def pass_copy(part, slot, group, offset):
        return pltpu.make_async_remote_copy(
            src_ref=full.at[group, slot, rows(part)], dst_ref=full.at[group, slot, rows(part)],
            send_sem=pass_out.at[part, offset, slot], recv_sem=pass_in.at[part, group, slot],
            device_id=(me, sibling(offset)), device_id_type=MESH,
        )

    def each_other(body):
        def step(offset, carry):
            body(other(offset))
            return carry

        lax.fori_loop(1, seq, step, 0)

    barrier = pltpu.get_barrier_semaphore()
    each_other(
        lambda peer: pl.semaphore_signal(barrier, inc=1, device_id=(peer, mine), device_id_type=MESH)
    )
    for offset in range(1, chan):
        pl.semaphore_signal(barrier, inc=1, device_id=(me, sibling(offset)), device_id_type=MESH)
    room = seq * each
    packed = [
        pltpu.make_async_copy(source, box, own.at[index])
        for index, (source, box) in enumerate(
            (
                (values, boxes_early.at[:, 0]),
                (gate_one, boxes_late.at[:, 0]),
                (gate_two, boxes_late.at[:, 1]),
            )
        )
    ]
    for copy in packed:
        copy.start()
    for taps, place, source, skip in (
        (boxes_early, 1, filter_one, skip_one),
        (boxes_late, 2, filter_two, skip_two),
    ):
        row = lax.broadcasted_iota(jnp.int32, (room, room), 0)
        lane = lax.broadcasted_iota(jnp.int32, (room, room), 1)
        column = jnp.sum(
            jnp.where(row == lane, jnp.broadcast_to(skip[...], (room, room)), 0.0), axis=1, keepdims=True
        )
        lane = lax.broadcasted_iota(jnp.int32, (room, LANES), 1)
        direct[...] = jnp.where(lane + me == 0, column, 0.0)

        def make_taps(target, carry, taps=taps, place=place, source=source):
            for tile in range(tiles):
                part = source[target, :, pl.ds(tile * LANES, LANES)]
                if tile == 0:
                    part = part + direct[pl.ds(target * each, each), :]
                taps[target, place, :, pl.ds(tile * LANES, LANES)] = part.astype(taps.dtype)
            return carry

        lax.fori_loop(0, seq, make_taps, 0)
    pl.semaphore_wait(barrier, seq - 1 + chan - 1)

    own_copies = [
        pltpu.make_async_copy(boxes[group].at[me], got[group].at[me], own.at[3 + group])
        for group in range(2)
    ]
    packed[0].wait()
    each_other(lambda peer: box_copy(0, peer, me).start())
    own_copies[0].start()
    packed[1].wait()
    packed[2].wait()
    each_other(lambda peer: box_copy(1, peer, me).start())
    own_copies[1].start()
    padded[pl.ds(0, lags), :] = jnp.zeros((lags, LANES), jnp.float32)

    def lay_out(group, first):
        each_other(lambda peer: box_copy(group, peer, peer).wait_recv())
        own_copies[group].wait()

        def step(source, carry):
            for index in range(got[group].shape[1]):
                block = got[group][source, index].astype(jnp.float32)
                for tile in range(tiles):
                    lines[first + index, rows_of(source * tiles + tile, each, lags), :] = block[
                        :, tile * LANES : (tile + 1) * LANES
                    ]
            return carry

        lax.fori_loop(0, seq, step, 0)

    def first_conv(channel, carry):
        base = pl.multiple_of(channel * lags, lags)
        padded[pl.ds(lags, lags), :] = lines[0, pl.ds(base, lags), :]
        lines[0, pl.ds(base, lags), :] = toeplitz_conv(padded, lines.at[1, pl.ds(base, lags)], lags)
        return carry

    lay_out(0, 0)
    lax.fori_loop(0, each, first_conv, 0)
    lay_out(1, 2)

    def second_conv(channel, carry):
        base = pl.multiple_of(channel * lags, lags)
        here = pl.ds(base, lags)
        padded[pl.ds(lags, lags), :] = lines[2, here, :] * lines[0, here, :]
        second = toeplitz_conv(padded, lines.at[4, here], lags)
        lines[0, here, :] = lines[3, here, :] * second
        return carry

    own_back = []
    for part in range(parts):
        lax.fori_loop(part * share, (part + 1) * share, second_conv, 0)

        def gather(target, carry, part=part):
            for tile in range(tiles):
                ready[target, rows(part), pl.ds(tile * LANES, LANES)] = lines[
                    0, rows_of(part * share * lags + target * tiles + tile, share, lags), :
                ].astype(ready.dtype)
            return carry

        lax.fori_loop(0, seq, gather, 0)
        each_other(lambda peer, part=part: back_copy(part, peer, me).start())
        own_back.append(
            pltpu.make_async_copy(
                ready.at[me, rows(part)], full.at[mine, me, rows(part)], own.at[5 + part]
            )
        )
        own_back[-1].start()

    def pass_on(part, slot):
        for offset in range(1, chan):
            pass_copy(part, slot, mine, offset).start()

    for part in range(parts):
        own_back[part].wait()
        pass_on(part, me)

        def arrived(peer, part=part):
            back_copy(part, peer, peer).wait_recv()
            pass_on(part, peer)

        each_other(arrived)

    def widen(group, slot):
        wide[pl.ds((group * seq + slot) * each, each), :] = full[group, slot].astype(jnp.float32)

    def widen_mine(slot, carry):
        widen(mine, slot)
        return carry

    lax.fori_loop(0, seq, widen_mine, 0)
    for offset in range(1, chan):
        group = sibling(offset)

        def widen_other(slot, carry, group=group, offset=offset):
            for part in range(parts):
                pass_copy(part, slot, group, offset).wait_recv()
            widen(group, slot)
            return carry

        lax.fori_loop(0, seq, widen_other, 0)

    out[...] = lax.dot_general(
        mix[...],
        wide[...].astype(jnp.bfloat16),
        (((0,), (0,)), ((), ())),
        preferred_element_type=jnp.float32,
    )

    for group in range(2):
        each_other(lambda peer, group=group: box_copy(group, peer, me).wait_send())
    for part in range(parts):
        each_other(lambda peer, part=part: back_copy(part, peer, me).wait_send())
        for offset in range(1, chan):

            def sent(slot, carry, part=part, offset=offset):
                pass_copy(part, slot, mine, offset).wait_send()
                return carry

            lax.fori_loop(0, seq, sent, 0)


def per_device(
    seq, chan, values, gate_one, gate_two, filter_one, filter_two, skip_one, skip_two, mix_weight
):
    channels, tokens = values.shape
    made = mix_weight.shape[1]
    each = -(-channels // seq)
    parts = math.gcd(each, PARTS)
    lags = seq * tokens // LANES
    room = each * seq

    def spread(source):
        return jnp.pad(source, ((0, room - channels), (0, 0))).reshape(seq, each, tokens)

    def lane_row(skip):
        return jnp.pad(skip, (0, room - channels)).reshape(1, room)

    mix = jnp.pad(
        mix_weight.reshape(chan, channels, made), ((0, 0), (0, room - channels), (0, 0))
    ).reshape(chan * room, made)
    anywhere = pl.BlockSpec(memory_space=pl.ANY)
    vmem = pl.BlockSpec(memory_space=pltpu.VMEM)
    dma = pltpu.SemaphoreType.DMA
    summed = pl.pallas_call(
        functools.partial(layer_kernel, seq, chan, each, parts, tokens),
        in_specs=[anywhere] * 3 + [vmem] * 5,
        out_specs=vmem,
        out_shape=jax.ShapeDtypeStruct((made, tokens), jnp.float32),
        scratch_shapes=[
            pltpu.VMEM((seq, 2, each, tokens), jnp.bfloat16),
            pltpu.VMEM((seq, 3, each, tokens), jnp.bfloat16),
            pltpu.VMEM((seq, 2, each, tokens), jnp.bfloat16),
            pltpu.VMEM((seq, 3, each, tokens), jnp.bfloat16),
            pltpu.VMEM((room, LANES), jnp.float32),
            pltpu.VMEM((5, each * lags, LANES), jnp.float32),
            pltpu.VMEM((2 * lags, LANES), jnp.float32),
            pltpu.VMEM((seq, each, tokens), jnp.bfloat16),
            pltpu.VMEM((chan, seq, each, tokens), jnp.bfloat16),
            pltpu.VMEM((chan * room, tokens), jnp.float32),
            dma((2, seq)),
            dma((2, seq)),
            dma((parts, seq)),
            dma((parts, seq)),
            dma((parts, chan, seq)),
            dma((parts, chan, seq)),
            dma((5 + parts,)),
        ],
        compiler_params=pltpu.CompilerParams(collective_id=0, has_side_effects=True),
    )(
        spread(values), spread(gate_one), spread(gate_two), spread(filter_one), spread(filter_two),
        lane_row(skip_one), lane_row(skip_two), mix,
    )
    return (summed / (1.0 + jnp.exp(-summed))).astype(jnp.bfloat16)


def solution(mesh):
    both = P("chan", "seq")
    return jax.shard_map(
        functools.partial(per_device, mesh.shape["seq"], mesh.shape["chan"]),
        mesh=mesh,
        in_specs=(both, both, both, both, both, P("chan"), P("chan"), P(None, "chan")),
        out_specs=both,
        check_vma=False,
    )
```

```python
import functools
import math

import jax
import jax.numpy as jnp
from jax import lax
from jax.experimental import pallas as pl
from jax.experimental.pallas import tpu as pltpu
from jax.sharding import PartitionSpec as P

LANES = 128
GROUP = 64
PARTS = 1
MESH = pl.DeviceIdType.MESH


def toeplitz_conv(padded, taps, lags):
    group_size = math.gcd(lags, GROUP)
    row = lax.broadcasted_iota(jnp.int32, (LANES, LANES), 0)
    lane = lax.broadcasted_iota(jnp.int32, (LANES, LANES), 1)
    lower = lane >= row

    def step(group, carry):
        total, before = carry
        left, right = [], []
        for inner in range(group_size):
            lag = group * group_size + inner
            line = jnp.broadcast_to(taps[pl.ds(lag, 1), :], (LANES, LANES))
            turned = pltpu.roll(line, 0, 1, stride=1, stride_axis=0)
            right.append(jnp.where(lower, turned, before).astype(jnp.bfloat16))
            before = turned
            left.append(padded[pl.ds(lags - lag, lags), :].astype(jnp.bfloat16))
        total = total + jnp.dot(
            jnp.concatenate(left, axis=1),
            jnp.concatenate(right, axis=0),
            preferred_element_type=jnp.float32,
        )
        return total, before

    start = (jnp.zeros((lags, LANES), jnp.float32), jnp.zeros((LANES, LANES), jnp.float32))
    if group_size == lags:
        return step(0, start)[0]
    return lax.fori_loop(0, lags // group_size, step, start)[0]


def rows_of(start, count, stride):
    return pl.ds(start, count, stride=stride) if count > 1 else pl.ds(start, 1)


def layer_kernel(
    seq, chan, each, parts, tokens,
    values, gate_one, gate_two, filter_one, filter_two, skip_one, skip_two, mix, out,
    boxes_early, boxes_late, got_early, got_late, direct, lines, padded, ready, full, wide,
    sent_out, sent_in, back_out, back_in, pass_out, pass_in, own,
):
    me, mine = lax.axis_index("seq"), lax.axis_index("chan")
    tiles = tokens // LANES
    lags = seq * tiles
    share = each // parts

    def other(offset):
        return lax.rem(me + offset, seq)

    def sibling(offset):
        return lax.rem(mine + offset, chan)

    def to_peer(source, target, sent, landed, peer):
        return pltpu.make_async_remote_copy(
            src_ref=source, dst_ref=target, send_sem=sent, recv_sem=landed,
            device_id=(peer, mine), device_id_type=MESH,
        )

    boxes, got = (boxes_early, boxes_late), (got_early, got_late)

    def rows(part):
        return pl.ds(part * share, share)

    def box_copy(group, peer, slot):
        return to_peer(
            boxes[group].at[peer], got[group].at[slot],
            sent_out.at[group, peer], sent_in.at[group, slot], peer,
        )

    def back_copy(part, peer, slot):
        return to_peer(
            ready.at[peer, rows(part)], full.at[mine, slot, rows(part)],
            back_out.at[part, peer], back_in.at[part, slot], peer,
        )

    def pass_copy(group, offset):
        return pltpu.make_async_remote_copy(
            src_ref=full.at[group], dst_ref=full.at[group],
            send_sem=pass_out.at[offset], recv_sem=pass_in.at[group],
            device_id=(me, sibling(offset)), device_id_type=MESH,
        )

    def each_other(body):
        def step(offset, carry):
            body(other(offset))
            return carry

        lax.fori_loop(1, seq, step, 0)

    barrier = pltpu.get_barrier_semaphore()
    each_other(
        lambda peer: pl.semaphore_signal(barrier, inc=1, device_id=(peer, mine), device_id_type=MESH)
    )
    for offset in range(1, chan):
        pl.semaphore_signal(barrier, inc=1, device_id=(me, sibling(offset)), device_id_type=MESH)
    room = seq * each
    packed = [
        pltpu.make_async_copy(source, box, own.at[index])
        for index, (source, box) in enumerate(
            (
                (values, boxes_early.at[:, 0]),
                (gate_one, boxes_late.at[:, 0]),
                (gate_two, boxes_late.at[:, 1]),
            )
        )
    ]
    for copy in packed:
        copy.start()
    for taps, place, source, skip in (
        (boxes_early, 1, filter_one, skip_one),
        (boxes_late, 2, filter_two, skip_two),
    ):
        row = lax.broadcasted_iota(jnp.int32, (room, room), 0)
        lane = lax.broadcasted_iota(jnp.int32, (room, room), 1)
        column = jnp.sum(
            jnp.where(row == lane, jnp.broadcast_to(skip[...], (room, room)), 0.0), axis=1, keepdims=True
        )
        lane = lax.broadcasted_iota(jnp.int32, (room, LANES), 1)
        direct[...] = jnp.where(lane + me == 0, column, 0.0)

        def make_taps(target, carry, taps=taps, place=place, source=source):
            for tile in range(tiles):
                part = source[target, :, pl.ds(tile * LANES, LANES)]
                if tile == 0:
                    part = part + direct[pl.ds(target * each, each), :]
                taps[target, place, :, pl.ds(tile * LANES, LANES)] = part.astype(taps.dtype)
            return carry

        lax.fori_loop(0, seq, make_taps, 0)
    pl.semaphore_wait(barrier, seq - 1 + chan - 1)

    own_copies = [
        pltpu.make_async_copy(boxes[group].at[me], got[group].at[me], own.at[3 + group])
        for group in range(2)
    ]
    packed[0].wait()
    each_other(lambda peer: box_copy(0, peer, me).start())
    own_copies[0].start()
    packed[1].wait()
    packed[2].wait()
    each_other(lambda peer: box_copy(1, peer, me).start())
    own_copies[1].start()
    padded[pl.ds(0, lags), :] = jnp.zeros((lags, LANES), jnp.float32)

    def lay_out(group, first):
        each_other(lambda peer: box_copy(group, peer, peer).wait_recv())
        own_copies[group].wait()

        def step(source, carry):
            for index in range(got[group].shape[1]):
                block = got[group][source, index].astype(jnp.float32)
                for tile in range(tiles):
                    lines[first + index, rows_of(source * tiles + tile, each, lags), :] = block[
                        :, tile * LANES : (tile + 1) * LANES
                    ]
            return carry

        lax.fori_loop(0, seq, step, 0)

    def first_conv(channel, carry):
        base = pl.multiple_of(channel * lags, lags)
        padded[pl.ds(lags, lags), :] = lines[0, pl.ds(base, lags), :]
        lines[0, pl.ds(base, lags), :] = toeplitz_conv(padded, lines.at[1, pl.ds(base, lags)], lags)
        return carry

    lay_out(0, 0)
    lax.fori_loop(0, each, first_conv, 0)
    lay_out(1, 2)

    def second_conv(channel, carry):
        base = pl.multiple_of(channel * lags, lags)
        here = pl.ds(base, lags)
        padded[pl.ds(lags, lags), :] = lines[2, here, :] * lines[0, here, :]
        second = toeplitz_conv(padded, lines.at[4, here], lags)
        lines[0, here, :] = lines[3, here, :] * second
        return carry

    own_back = []
    for part in range(parts):
        lax.fori_loop(part * share, (part + 1) * share, second_conv, 0)

        def gather(target, carry, part=part):
            for tile in range(tiles):
                ready[target, rows(part), pl.ds(tile * LANES, LANES)] = lines[
                    0, rows_of(part * share * lags + target * tiles + tile, share, lags), :
                ].astype(ready.dtype)
            return carry

        lax.fori_loop(0, seq, gather, 0)
        each_other(lambda peer, part=part: back_copy(part, peer, me).start())
        own_back.append(
            pltpu.make_async_copy(
                ready.at[me, rows(part)], full.at[mine, me, rows(part)], own.at[5 + part]
            )
        )
        own_back[-1].start()

    for part in range(parts):
        own_back[part].wait()
        each_other(lambda peer, part=part: back_copy(part, peer, peer).wait_recv())
    for offset in range(1, chan):
        pass_copy(mine, offset).start()

    def widen(group, slot):
        wide[pl.ds((group * seq + slot) * each, each), :] = full[group, slot].astype(jnp.float32)

    def widen_mine(slot, carry):
        widen(mine, slot)
        return carry

    lax.fori_loop(0, seq, widen_mine, 0)
    for offset in range(1, chan):
        group = sibling(offset)
        pass_copy(group, offset).wait_recv()

        def widen_other(slot, carry, group=group, offset=offset):
            widen(group, slot)
            return carry

        lax.fori_loop(0, seq, widen_other, 0)

    out[...] = lax.dot_general(
        mix[...],
        wide[...].astype(jnp.bfloat16),
        (((0,), (0,)), ((), ())),
        preferred_element_type=jnp.float32,
    )

    for group in range(2):
        each_other(lambda peer, group=group: box_copy(group, peer, me).wait_send())
    for part in range(parts):
        each_other(lambda peer, part=part: back_copy(part, peer, me).wait_send())
    for offset in range(1, chan):
        pass_copy(mine, offset).wait_send()


def per_device(
    seq, chan, values, gate_one, gate_two, filter_one, filter_two, skip_one, skip_two, mix_weight
):
    channels, tokens = values.shape
    made = mix_weight.shape[1]
    each = -(-channels // seq)
    parts = math.gcd(each, PARTS)
    lags = seq * tokens // LANES
    room = each * seq

    def spread(source):
        return jnp.pad(source, ((0, room - channels), (0, 0))).reshape(seq, each, tokens)

    def lane_row(skip):
        return jnp.pad(skip, (0, room - channels)).reshape(1, room)

    mix = jnp.pad(
        mix_weight.reshape(chan, channels, made), ((0, 0), (0, room - channels), (0, 0))
    ).reshape(chan * room, made)
    anywhere = pl.BlockSpec(memory_space=pl.ANY)
    vmem = pl.BlockSpec(memory_space=pltpu.VMEM)
    dma = pltpu.SemaphoreType.DMA
    summed = pl.pallas_call(
        functools.partial(layer_kernel, seq, chan, each, parts, tokens),
        in_specs=[anywhere] * 3 + [vmem] * 5,
        out_specs=vmem,
        out_shape=jax.ShapeDtypeStruct((made, tokens), jnp.float32),
        scratch_shapes=[
            pltpu.VMEM((seq, 2, each, tokens), jnp.bfloat16),
            pltpu.VMEM((seq, 3, each, tokens), jnp.bfloat16),
            pltpu.VMEM((seq, 2, each, tokens), jnp.bfloat16),
            pltpu.VMEM((seq, 3, each, tokens), jnp.bfloat16),
            pltpu.VMEM((room, LANES), jnp.float32),
            pltpu.VMEM((5, each * lags, LANES), jnp.float32),
            pltpu.VMEM((2 * lags, LANES), jnp.float32),
            pltpu.VMEM((seq, each, tokens), jnp.bfloat16),
            pltpu.VMEM((chan, seq, each, tokens), jnp.bfloat16),
            pltpu.VMEM((chan * room, tokens), jnp.float32),
            dma((2, seq)),
            dma((2, seq)),
            dma((parts, seq)),
            dma((parts, seq)),
            dma((chan,)),
            dma((chan,)),
            dma((5 + parts,)),
        ],
        compiler_params=pltpu.CompilerParams(collective_id=0, has_side_effects=True),
    )(
        spread(values), spread(gate_one), spread(gate_two), spread(filter_one), spread(filter_two),
        lane_row(skip_one), lane_row(skip_two), mix,
    )
    return (summed / (1.0 + jnp.exp(-summed))).astype(jnp.bfloat16)


def solution(mesh):
    both = P("chan", "seq")
    return jax.shard_map(
        functools.partial(per_device, mesh.shape["seq"], mesh.shape["chan"]),
        mesh=mesh,
        in_specs=(both, both, both, both, both, P("chan"), P("chan"), P(None, "chan")),
        out_specs=both,
        check_vma=False,
    )
```
